512 devices in a mesh: section: 4 (over x), ctx: 64 (over y_lo, z, core), tp: 2 (over y_hi).
Axes of the slice: x: 4, y: 4 (y_hi: 2, y_lo: 2; y = y_hi * 2 + y_lo), z: 16, core: 2. Of those that a mesh axis runs over, the one named last changes fastest.
Arguments:
- video_feats: bfloat16 [8192, 1024], P('ctx', ('section', 'tp')), may hold values from -512 to 512
- ir_feats: bfloat16 [2048, 768], P('ctx', ('section', 'tp')), may hold values from -512 to 512
- video_adapter: bfloat16 [1024, 8, 768], P(('section', 'tp')), may hold values from -0.1875 to 0.1875
- ir_adapter: bfloat16 [768, 8, 768], P(('section', 'tp')), may hold values from -0.21875 to 0.21875
- text_query: bfloat16 [6144, 4096], P('ctx', ('section', 'tp')), may hold values from -4.5 to 4.5
- text_key: bfloat16 [6144, 1024], P('ctx', ('section', 'tp')), may hold values from -4.5 to 4.5
- text_value: bfloat16 [6144, 1024], P('ctx', ('section', 'tp')), may hold values from -6 to 6
- frame_live_counts: int32 [64, 2], replicated, may hold values from 1 to 128, as said below
- block_mask: int32 [64, 64], replicated, may hold values from 0 to 1, as said below
Outputs:
- attended: bfloat16 [16384, 4096], P('ctx', ('section', 'tp'))
The draws below stay inside these ranges and needn't reach their ends.
Inputs may be any that keep to these rules, and one draw needn't show every extreme that they name: frame_live_counts[f][0] of the 128 video slots and frame_live_counts[f][1] of the 32 IR slots of frame f are live, the first ones of each; some frame has all of its slots live. block_mask[b][c] is 1 where c = b and 0 where c > b.
All inputs are finite; a program needn't handle non-finite values.
Results may differ from the reference program's by a relative error of at most 0.02.
Values may be sent and summed in bfloat16 or wider, within the bound.
A program may use at most 64 MiB of HBM per device.

```python
import jax
import jax.numpy as jnp
from jax import lax

HEADS = 32
KV_HEADS = 8
HEAD_DIM = 128
D_VID = 1024
D_IR = 768
VTOK = 128
ITOK = 32
XTOK = 96
QPK = 4
GW = 768
BLK = 256
FRAMES = 64


def feature_draw(base_key, row_count, feature_count):
    first, second, third = jax.random.split(base_key, 3)
    column = jnp.arange(feature_count, dtype=jnp.float32) / (feature_count - 1)
    column_scale = 10.0 ** column * jax.random.uniform(first, (feature_count,), jnp.float32, 0.7, 1.4)
    row_shift = jax.random.uniform(second, (row_count, 1), jnp.float32, -1.0, 1.0)
    ramp = 2.0 * column
    noise = jnp.clip(jax.random.normal(third, (row_count, feature_count), jnp.float32), -4.0, 4.0)
    result = column_scale * (noise + row_shift * ramp)
    return result.astype(jnp.bfloat16)


def draw_video_feats(key, part):
    return feature_draw(jax.random.fold_in(key, 11), VTOK * FRAMES, D_VID)


def draw_ir_feats(key, part):
    return feature_draw(jax.random.fold_in(key, 17), ITOK * FRAMES, D_IR)


def text_draw(key):
    base_key = jax.random.fold_in(key, 29)
    query_key, key_key = jax.random.split(base_key, 2)
    row_count = XTOK * FRAMES
    query_part = jnp.clip(jax.random.normal(query_key, (row_count, HEADS * HEAD_DIM), jnp.float32), -4.5, 4.5)
    key_part = jnp.clip(jax.random.normal(key_key, (row_count, KV_HEADS * HEAD_DIM), jnp.float32), -4.5, 4.5)
    return (query_part, key_part)


def draw_text_query(key, part):
    return text_draw(key)[0].astype(jnp.bfloat16)


def draw_text_key(key, part):
    return text_draw(key)[1].astype(jnp.bfloat16)


def draw_frame_live_counts(key, part):
    base_key = jax.random.fold_in(key, 43)
    first, second, third, fourth = jax.random.split(base_key, 4)
    video_count = jax.random.randint(first, (FRAMES,), 1, VTOK + 1)
    ir_count = jax.random.randint(second, (FRAMES,), 1, ITOK + 1)
    full_frame = jax.random.randint(third, (), 0, FRAMES)
    sparse_frame = (full_frame + 1 + jax.random.randint(fourth, (), 0, FRAMES - 1)) % FRAMES
    frame_ids = jnp.arange(FRAMES, dtype=jnp.int32)
    video_count = jnp.where(frame_ids == full_frame, VTOK, jnp.where(frame_ids == sparse_frame, 1, video_count))
    ir_count = jnp.where(frame_ids == full_frame, ITOK, jnp.where(frame_ids == sparse_frame, 1, ir_count))
    return jnp.stack([video_count, ir_count], axis=1).astype(jnp.int32)


def draw_block_mask(key, part):
    coin = jax.random.randint(jax.random.fold_in(key, 57), (FRAMES, FRAMES), 0, 2)
    row_ids = jnp.arange(FRAMES, dtype=jnp.int32)[:, None]
    column_ids = jnp.arange(FRAMES, dtype=jnp.int32)[None, :]
    return jnp.where(row_ids == column_ids, 1, jnp.where(column_ids < row_ids, coin, 0)).astype(jnp.int32)


def block_scale(key, dims, shards, least, top_value):
    gain = 1.0
    for position, parts in shards:
        steps = jax.random.uniform(jax.random.fold_in(jax.random.fold_in(key, 6), position), (parts,), jnp.float32, least / len(shards), top_value / len(shards))
        gain = gain * jnp.repeat(jnp.exp(steps), dims[position] // parts).reshape((-1,) + (1,) * (len(dims) - 1 - position))
    return gain


def scatter_about(key, dims, width, reach, cuts=(), kind=jnp.bfloat16):
    values = width * jax.random.normal(key, dims, jnp.float32)
    if cuts:
        values = values * block_scale(key, dims, cuts, -0.22, 0.18)
    return jnp.clip(values, -reach, reach).astype(kind)


def setup_inputs(seed: int = 0) -> dict:
    streams_of = jax.random.split(jax.random.key(seed), 10)
    video_feats = draw_video_feats(jax.random.fold_in(streams_of[9], 71), 0)
    ir_feats = draw_ir_feats(jax.random.fold_in(streams_of[9], 71), 0)
    video_adapter = scatter_about(streams_of[2], (D_VID, KV_HEADS, GW), D_VID ** -0.5, 0.1875, ((0, 8),))
    ir_adapter = scatter_about(streams_of[3], (D_IR, KV_HEADS, GW), D_IR ** -0.5, 0.21875, ((0, 8),))
    text_query = draw_text_query(jax.random.fold_in(streams_of[9], 71), 0)
    text_key = draw_text_key(jax.random.fold_in(streams_of[9], 71), 0)
    text_value = scatter_about(streams_of[6], (XTOK * FRAMES, KV_HEADS * HEAD_DIM), 1.0, 6.0, ((0, 64), (1, 8)))
    frame_live_counts = draw_frame_live_counts(jax.random.fold_in(streams_of[9], 71), 0)
    block_mask = draw_block_mask(jax.random.fold_in(streams_of[9], 71), 0)
    return dict(video_feats=video_feats, ir_feats=ir_feats, video_adapter=video_adapter, ir_adapter=ir_adapter, text_query=text_query, text_key=text_key, text_value=text_value, frame_live_counts=frame_live_counts, block_mask=block_mask)


LN_EPSILON = 1e-05
NEG_LARGE = -1e+30

def layer_normed(feature_block):
    values = feature_block.astype(jnp.float32)
    center = lax.optimization_barrier(jnp.mean(values, axis=-1, keepdims=True))
    spread = lax.optimization_barrier(jnp.mean(values * values, axis=-1, keepdims=True)) - center * center
    return ((values - center) * lax.rsqrt(spread + LN_EPSILON)).astype(jnp.bfloat16)

def key_alive_flags(frame_lookup, frame_live_counts):
    slot_index = jnp.arange(BLK, dtype=jnp.int32)
    video_live = slot_index < frame_live_counts[frame_lookup, 0]
    ir_live = slot_index - VTOK < frame_live_counts[frame_lookup, 1]
    return jnp.where(slot_index < VTOK, video_live, jnp.where(slot_index < VTOK + ITOK, ir_live, True))

def reference(video_feats, ir_feats, video_adapter, ir_adapter, text_query, text_key, text_value, frame_live_counts, block_mask):
    query_width = QPK * HEAD_DIM
    video_proj = jnp.dot(layer_normed(video_feats), video_adapter.reshape(D_VID, KV_HEADS * GW), preferred_element_type=jnp.float32).astype(jnp.bfloat16).reshape(FRAMES, VTOK, KV_HEADS, GW)
    ir_proj = jnp.dot(layer_normed(ir_feats), ir_adapter.reshape(D_IR, KV_HEADS * GW), preferred_element_type=jnp.float32).astype(jnp.bfloat16).reshape(FRAMES, ITOK, KV_HEADS, GW)
    joint_query = jnp.concatenate([video_proj[..., :query_width], ir_proj[..., :query_width], text_query.reshape(FRAMES, XTOK, KV_HEADS, query_width)], axis=1)
    joint_key = jnp.concatenate([video_proj[..., query_width:query_width + HEAD_DIM], ir_proj[..., query_width:query_width + HEAD_DIM], text_key.reshape(FRAMES, XTOK, KV_HEADS, HEAD_DIM)], axis=1)
    joint_value = jnp.concatenate([video_proj[..., query_width + HEAD_DIM:], ir_proj[..., query_width + HEAD_DIM:], text_value.reshape(FRAMES, XTOK, KV_HEADS, HEAD_DIM)], axis=1)
    scale = HEAD_DIM ** (-0.5)
    query_count = BLK * QPK

    def one_pair(pair_index):
        kv_group = pair_index // FRAMES
        query_frame = pair_index % FRAMES
        query_rows = joint_query[query_frame, :, kv_group].reshape(query_count, HEAD_DIM)
        query_position = query_frame * BLK + jnp.arange(query_count, dtype=jnp.int32) // QPK

        def scores_for(key_frame_ids):
            key_block = joint_key[key_frame_ids, :, kv_group]
            scores = jnp.dot(query_rows, key_block.T, preferred_element_type=jnp.float32) * scale
            key_position = key_frame_ids * BLK + jnp.arange(BLK, dtype=jnp.int32)
            permitted_mask = (key_position[None, :] <= query_position[:, None]) & key_alive_flags(key_frame_ids, frame_live_counts)[None, :]
            return (scores, permitted_mask)

        def visible(key_frame_ids):
            return (block_mask[query_frame, key_frame_ids] == 1) & (key_frame_ids <= query_frame)

        def max_step(key_frame_ids, row_top):

            def found(row_top):
                scores, permitted_mask = scores_for(key_frame_ids)
                return jnp.maximum(row_top, lax.optimization_barrier(jnp.max(jnp.where(permitted_mask, scores, NEG_LARGE), axis=1)))
            return lax.cond(visible(key_frame_ids), found, lambda kept: kept, row_top)
        row_top = lax.fori_loop(0, FRAMES, max_step, jnp.full((query_count,), NEG_LARGE, jnp.float32))

        def sum_step(key_frame_ids, state_now):

            def found(state_now):
                row_sums, weighted = state_now
                scores, permitted_mask = scores_for(key_frame_ids)
                weights = jnp.where(permitted_mask, jnp.exp(scores - row_top[:, None]), 0.0)
                row_sums = row_sums + lax.optimization_barrier(jnp.sum(weights, axis=1))
                weighted = weighted + jnp.dot(weights.astype(jnp.bfloat16), joint_value[key_frame_ids, :, kv_group], preferred_element_type=jnp.float32)
                return (row_sums, weighted)
            return lax.cond(visible(key_frame_ids), found, lambda kept: kept, state_now)
        row_sums, weighted = lax.fori_loop(0, FRAMES, sum_step, (jnp.zeros((query_count,), jnp.float32), jnp.zeros((query_count, HEAD_DIM), jnp.float32)))
        return (weighted / row_sums[:, None]).astype(jnp.bfloat16)
    outputs = lax.map(one_pair, jnp.arange(KV_HEADS * FRAMES, dtype=jnp.int32))
    outputs = outputs.reshape(KV_HEADS, FRAMES, BLK, QPK, HEAD_DIM).transpose(1, 2, 0, 3, 4)
    return outputs.reshape(FRAMES * BLK, HEADS * HEAD_DIM)
```

```python
import functools

import jax
import jax.numpy as jnp
from jax import lax
from jax.experimental import pallas as pl
from jax.experimental.pallas import tpu as pltpu
from jax.sharding import PartitionSpec as P

HEAD_DIM = 128
D_VID = 1024
D_IR = 768
VTOK = 128
ITOK = 32
ENC = VTOK + ITOK
XTOK = 96
QPK = 4
QW = QPK * HEAD_DIM
GW = 768
KVW = 2 * HEAD_DIM
BLK = 256
PAIR = 2 * BLK

LN_EPSILON = 1e-05
NEG_LARGE = -1e30
LOG2E = 1.4426950408889634
MESH = pl.DeviceIdType.MESH

PIECES = ((ENC, XTOK), (0, ENC // 2), (ENC // 2, ENC // 2))
TEXT, FIRST, SECOND = 0, 1, 2
PROJ_TICK = 4
STREAMS = ((TEXT, 0), (FIRST, PROJ_TICK), (SECOND, PROJ_TICK), (SECOND, PROJ_TICK + 1))
LAG = 2


def kernel(
    n_section,
    n_ctx,
    n_tp,
    vf_ref,
    if_ref,
    wv_ref,
    wi_ref,
    tq_ref,
    tk_ref,
    tv_ref,
    counts_ref,
    mask_ref,
    out_ref,
    kv,
    bias,
    xv,
    xi,
    wvb,
    wib,
    qa,
    top,
    acc,
    kv_recv,
    z_send,
    core_send,
    y_send,
    yc_send,
    x_recv,
    x_send,
    w_recv,
    w_send,
    w_fwd,
    local_sem,
):
    section = lax.axis_index("section")
    ctx = lax.axis_index("ctx")
    tp = lax.axis_index("tp")
    n_z = n_ctx // 4
    half = n_z // 2
    row = ctx // (2 * n_z)
    z = (ctx // 2) % n_z
    core = ctx % 2
    shard = section * n_tp + tp
    n_shard = n_section * n_tp

    def frame_at(r, zz, k):
        return r * (2 * n_z) + zz * 2 + k

    core_peer = {"ctx": frame_at(row, z, 1 - core)}
    y_peer = {"ctx": frame_at(1 - row, z, core)}
    z_peer = (
        {"ctx": frame_at(row, (z + 1) % n_z, core)},
        {"ctx": frame_at(row, (z + n_z - 1) % n_z, core)},
    )
    others = [(a, b) for a in range(n_section) for b in range(n_tp) if (a, b) != (0, 0)]

    def feature_peer(a, b):
        return {"section": (section + a) % n_section, "tp": (tp + b) % n_tp}

    def weight_peer(a, b):
        peer = feature_peer(a, b)
        if b:
            peer["ctx"] = frame_at(1 - row, z, core)
        return peer

    barrier = pltpu.get_barrier_semaphore()
    greeted = [core_peer, y_peer, z_peer[0], z_peer[1]]
    greeted += [feature_peer(a, b) for a, b in others]
    greeted += [weight_peer(a, b) for a, b in others if b]
    for peer in greeted:
        pl.semaphore_signal(barrier, inc=1, device_id=peer, device_id_type=MESH)

    own_rows = pl.multiple_of(ctx * BLK, BLK)
    own_group = shard
    v_half, i_half = D_VID // n_shard // 2, D_IR // n_shard // 2
    v_rows, i_rows = 2 * v_half, 2 * i_half
    locals_ = [
        pltpu.make_async_copy(tk_ref, kv.at[pl.ds(own_rows + ENC, XTOK), pl.ds(0, HEAD_DIM)], local_sem.at[0]),
        pltpu.make_async_copy(tv_ref, kv.at[pl.ds(own_rows + ENC, XTOK), pl.ds(HEAD_DIM, HEAD_DIM)], local_sem.at[1]),
        pltpu.make_async_copy(vf_ref, xv.at[:, pl.ds(pl.multiple_of(shard * 128, 128), 128)], local_sem.at[2]),
        pltpu.make_async_copy(if_ref, xi.at[shard], local_sem.at[3]),
        pltpu.make_async_copy(wv_ref.at[own_group], wvb.at[pl.ds(pl.multiple_of(shard * v_rows, v_rows), v_rows)], local_sem.at[4]),
        pltpu.make_async_copy(wi_ref.at[own_group], wib.at[shard], local_sem.at[5]),
    ]
    for copy in locals_:
        copy.start()

    def remote(src, dst, send_sem, recv_sem, peer):
        return pltpu.make_async_remote_copy(
            src_ref=src, dst_ref=dst, send_sem=send_sem, recv_sem=recv_sem, device_id=peer, device_id_type=MESH
        )

    def feature_sends(n):
        peer = feature_peer(*others[n])
        columns = pl.ds(pl.multiple_of(shard * 128, 128), 128)
        return [
            remote(vf_ref, xv.at[:, columns], x_send.at[0, n], x_recv.at[0, shard], peer),
            remote(if_ref, xi.at[shard], x_send.at[1, n], x_recv.at[1, shard], peer),
        ]

    parts = (pl.ds(QW, KVW), pl.ds(0, QW))

    def weight_places(src_shard, k, part):
        v_at = pl.ds(pl.multiple_of(src_shard * v_rows + k * v_half, v_half), v_half)
        i_at = pl.ds(pl.multiple_of(k * i_half, i_half), i_half)
        return wvb.at[v_at, parts[part]], wib.at[src_shard, i_at, parts[part]]

    def weight_sends(n, part):
        a, b = others[n]
        group = ((section + a) % n_section) * n_tp + (tp + b) % n_tp
        v_dst, i_dst = weight_places(shard, core, part)
        v_at = pl.ds(pl.multiple_of(core * v_half, v_half), v_half)
        i_at = pl.ds(pl.multiple_of(core * i_half, i_half), i_half)
        peer = weight_peer(a, b)
        return [
            remote(wv_ref.at[group, v_at, parts[part]], v_dst, w_send.at[0, part, n], w_recv.at[0, part, 0, shard], peer),
            remote(wi_ref.at[group, i_at, parts[part]], i_dst, w_send.at[1, part, n], w_recv.at[1, part, 0, shard], peer),
        ]

    def weight_forwards(n, part):
        a, b = others[n]
        src_shard = ((section + a) % n_section) * n_tp + (tp + b) % n_tp
        places = weight_places(src_shard, core, part)
        return [
            remote(place, place, w_fwd.at[i, part, n], w_recv.at[i, part, 1, src_shard], core_peer)
            for i, place in enumerate(places)
        ]

    def weight_arrivals(n, part, hop):
        a, b = others[n]
        src_shard = ((section + a) % n_section) * n_tp + (tp + b) % n_tp
        places = weight_places(src_shard, core if hop == 0 else 1 - core, part)
        return [
            remote(place, place, w_fwd.at[i, part, n], w_recv.at[i, part, hop, src_shard], core_peer)
            for i, place in enumerate(places)
        ]

    def piece_at(frame, piece):
        first, count = PIECES[piece]
        return kv.at[pl.ds(pl.multiple_of(frame * BLK + first, 16), count)]

    def arrived(frame, piece):
        place = piece_at(frame, piece)
        remote(place, place, z_send.at[0, 0, 0], kv_recv.at[frame, piece], core_peer).wait_recv()

    def send(frame, piece, sem, peer):
        place = piece_at(frame, piece)
        return remote(place, place, sem, kv_recv.at[frame, piece], peer)

    def reach(way):
        return half - core if way == 0 else half - 1 + core

    def z_of(way, distance):
        return (z + n_z - distance) % n_z if way == 0 else (z + distance) % n_z

    def act(copy, start):
        if start:
            copy.start()
        else:
            copy.wait_send()

    def line_step(tick, way, stream, start):
        piece, offset = STREAMS[stream]
        distance = tick - offset
        slot = tick % 2
        frame = frame_at(0 if stream == 3 else row, z_of(way, (distance + n_z) % n_z), core)
        active = (distance >= 0) & (distance <= reach(way))
        if stream == 3:
            active = active & (row == 1)

        @pl.when(active)
        def _():
            if start:
                if stream == 3 and way == 0:
                    arrived(frame, piece)
                else:
                    @pl.when(distance >= 1)
                    def _():
                        arrived(frame, piece)

            @pl.when(distance < reach(way))
            def _():
                act(send(frame, piece, z_send.at[way, stream, slot], z_peer[way]), start)

            if way == 0:
                act(send(frame, piece, core_send.at[way, stream, slot], core_peer), start)
            else:
                @pl.when(distance >= 1)
                def _():
                    act(send(frame, piece, core_send.at[way, stream, slot], core_peer), start)

            if stream in (0, 1):
                crosses = row == 0
                if way == 1:
                    crosses = crosses & (distance >= 1)
            elif stream == 2 and way == 0:
                crosses = (row == 0) & (distance == 0)
            else:
                crosses = None
            if crosses is not None:
                @pl.when(crosses)
                def _():
                    act(send(frame, piece, y_send.at[way, stream, slot], y_peer), start)

    def cross_step(tick, way, stream, start):
        piece, offset = STREAMS[stream]
        distance = tick - offset - 1
        slot = tick % 2
        frame = frame_at(0, z_of(way, (distance + n_z) % n_z), core)
        least = 0 if way == 0 else 1

        @pl.when((row == 1) & (distance >= least) & (distance <= reach(way)))
        def _():
            if start:
                arrived(frame, piece)
            act(send(frame, piece, yc_send.at[way, stream, slot], core_peer), start)

    def relay(tick, start=True):
        for stream in range(4):
            for way in range(2):
                line_step(tick, way, stream, start)
        for stream in range(2):
            for way in range(2):
                cross_step(tick, way, stream, start)

    def step(tick):
        relay(tick - 2, start=False)
        relay(tick)

    def attend(first_frame, diagonal):
        rows = pl.ds(pl.multiple_of(first_frame * BLK, PAIR), PAIR)
        keys = jnp.concatenate([kv[rows, :HEAD_DIM], bias[rows, :]], axis=1)
        values = jnp.concatenate([kv[rows, HEAD_DIM:], jnp.ones((PAIR, HEAD_DIM), jnp.bfloat16)], axis=1)
        for h in range(QPK):
            scores = lax.dot_general(
                qa[h], keys, (((1,), (1,)), ((), ())), preferred_element_type=jnp.float32
            )
            if diagonal:
                key_slot = lax.broadcasted_iota(jnp.int32, (BLK, PAIR), 1)
                query_slot = lax.broadcasted_iota(jnp.int32, (BLK, PAIR), 0) + core * BLK
                scores = jnp.where(key_slot <= query_slot, scores, NEG_LARGE)
            old = top[h]
            new = jnp.maximum(old, jnp.max(scores, axis=1, keepdims=True))
            top[h] = new
            weights = jnp.concatenate(
                [jnp.exp2(scores[:, i : i + HEAD_DIM] - new) for i in range(0, PAIR, HEAD_DIM)], axis=1
            ).astype(jnp.bfloat16)
            factor = jnp.exp2(old - new)
            acc[h] = acc[h] * jnp.concatenate([factor, factor], axis=1) + jnp.dot(
                weights, values, preferred_element_type=jnp.float32
            )

    def compute(distance):
        def item(n, _):
            way, r = n // 2, n % 2
            zz = jnp.where(way == 0, z + n_z - distance, z + distance) % n_z
            present = (r <= row) & (distance <= half) & ((way == 0) | ((distance >= 1) & (distance < half)))
            mine = (r == row) & (distance == 0)
            present = present & jnp.logical_not(mine)

            @pl.when(present)
            def _():
                for piece in range(3):
                    arrived(frame_at(r, zz, 1 - core), piece)

                @pl.when((r < row) | (zz < z))
                def _():
                    attend(frame_at(r, zz, 0), False)

            return 0

        lax.fori_loop(0, 4, item, 0)

    pl.semaphore_wait(barrier, len(greeted))
    locals_[0].wait()
    locals_[1].wait()
    for n in range(len(others)):
        for copy in feature_sends(n):
            copy.start()
    relay(0)
    for part in range(2):
        for n in range(len(others)):
            for copy in weight_sends(n, part):
                copy.start()

    def mask_frame(f, _):
        seen = mask_ref[ctx, f]
        video_live = counts_ref[f, 0] * seen
        ir_live = counts_ref[f, 1] * seen
        text_live = XTOK * seen
        base = pl.multiple_of(f * BLK, BLK)
        for first, count, live in ((0, VTOK, video_live), (VTOK, ITOK, ir_live), (ENC, XTOK, text_live)):
            slot = lax.broadcasted_iota(jnp.int32, (count, HEAD_DIM), 0)
            bias[pl.ds(base + first, count), :] = jnp.where(slot < live, 0.0, NEG_LARGE).astype(jnp.bfloat16)
        return 0

    lax.fori_loop(0, n_ctx, mask_frame, 0)

    for h in range(QPK):
        lane = lax.broadcasted_iota(jnp.int32, (BLK, HEAD_DIM), 1)
        qa[h, :, HEAD_DIM:] = jnp.where(lane == 0, 1.0, 0.0).astype(jnp.bfloat16)
        top[h] = jnp.full((BLK, HEAD_DIM), NEG_LARGE, jnp.float32)
        acc[h] = jnp.zeros((BLK, 2 * HEAD_DIM), jnp.float32)

    def early(tick, _):
        step(tick)
        return 0

    lax.fori_loop(1, PROJ_TICK, early, 0)

    for copy in locals_[2:]:
        copy.wait()
    for n in range(len(others)):
        a, b = others[n]
        src_shard = ((section + a) % n_section) * n_tp + (tp + b) % n_tp
        columns = pl.ds(pl.multiple_of(src_shard * 128, 128), 128)
        remote(xv.at[:, columns], xv.at[:, columns], x_send.at[0, n], x_recv.at[0, src_shard], core_peer).wait_recv()
        remote(xi.at[src_shard], xi.at[src_shard], x_send.at[1, n], x_recv.at[1, src_shard], core_peer).wait_recv()

    def norm_terms(total, squares, count):
        center = total / count
        spread = squares / count - center * center
        return center, lax.rsqrt(spread + LN_EPSILON)

    video = xv[...].astype(jnp.float32)
    center, gain = norm_terms(
        jnp.sum(video, axis=1, keepdims=True), jnp.sum(video * video, axis=1, keepdims=True), D_VID
    )
    xv[...] = ((video - center) * gain).astype(jnp.bfloat16)
    infra = [xi[n].astype(jnp.float32) for n in range(n_shard)]
    total = sum(jnp.sum(x, axis=1, keepdims=True) for x in infra)
    squares = sum(jnp.sum(x * x, axis=1, keepdims=True) for x in infra)
    center, gain = norm_terms(total, squares, D_IR)
    for n in range(n_shard):
        xi[n] = ((infra[n] - center) * gain).astype(jnp.bfloat16)

    def take_weights(part):
        for n in range(len(others)):
            for arrival, forward in zip(weight_arrivals(n, part, 0), weight_forwards(n, part)):
                arrival.wait_recv()
                forward.start()
        for n in range(len(others)):
            for arrival in weight_arrivals(n, part, 1):
                arrival.wait_recv()

    def project(columns):
        video_out = jnp.dot(xv[...], wvb[:, columns], preferred_element_type=jnp.float32)
        ir_out = sum(
            jnp.dot(xi[n], wib[n, :, columns], preferred_element_type=jnp.float32) for n in range(n_shard)
        )
        return video_out, ir_out

    take_weights(0)
    video_out, ir_out = project(slice(QW, GW))
    kv[pl.ds(own_rows, VTOK), :] = video_out.astype(jnp.bfloat16)
    kv[pl.ds(own_rows + VTOK, ITOK), :] = ir_out.astype(jnp.bfloat16)

    lax.fori_loop(PROJ_TICK, PROJ_TICK + 2 + LAG, early, 0)

    take_weights(1)
    scale = HEAD_DIM ** (-0.5) * LOG2E
    video_out, ir_out = project(slice(0, QW))
    for h in range(QPK):
        columns = slice(h * HEAD_DIM, (h + 1) * HEAD_DIM)
        qa[h, :VTOK, :HEAD_DIM] = (video_out[:, columns] * scale).astype(jnp.bfloat16)
        qa[h, VTOK:ENC, :HEAD_DIM] = (ir_out[:, columns] * scale).astype(jnp.bfloat16)
        qa[h, ENC:, :HEAD_DIM] = (tq_ref[:, columns].astype(jnp.float32) * scale).astype(jnp.bfloat16)

    for piece in range(3):
        arrived(frame_at(row, z, 1 - core), piece)
    attend(frame_at(row, z, 0), True)

    def late(tick, _):
        step(tick)
        compute(tick - PROJ_TICK - 2 - LAG)
        return 0

    last = half + PROJ_TICK + 3 + LAG
    lax.fori_loop(PROJ_TICK + 2 + LAG, last, late, 0)

    for h in range(QPK):
        out_ref[:, h * HEAD_DIM : (h + 1) * HEAD_DIM] = (
            acc[h, :, :HEAD_DIM] / acc[h, :, HEAD_DIM:]
        ).astype(jnp.bfloat16)

    relay(last - 2, start=False)
    relay(last - 1, start=False)
    for n in range(len(others)):
        for copy in feature_sends(n):
            copy.wait_send()
        for part in range(2):
            for copy in weight_sends(n, part) + weight_forwards(n, part):
                copy.wait_send()


def solution(mesh):
    n_section, n_ctx, n_tp = mesh.shape["section"], mesh.shape["ctx"], mesh.shape["tp"]
    n_shard = n_section * n_tp

    def shards(vf, irf, wv, wi, tq, tk, tv, counts, mask):
        anywhere = pl.BlockSpec(memory_space=pl.ANY)
        vmem = pl.BlockSpec(memory_space=pltpu.VMEM)
        smem = pl.BlockSpec(memory_space=pltpu.SMEM)
        dma = pltpu.SemaphoreType.DMA
        return pl.pallas_call(
            functools.partial(kernel, n_section, n_ctx, n_tp),
            out_shape=jax.ShapeDtypeStruct((BLK, QW), jnp.bfloat16),
            in_specs=[anywhere] * 4 + [vmem] + [anywhere] * 2 + [smem] * 2,
            out_specs=vmem,
            scratch_shapes=[
                pltpu.VMEM((n_ctx * BLK, KVW), jnp.bfloat16),
                pltpu.VMEM((n_ctx * BLK, HEAD_DIM), jnp.bfloat16),
                pltpu.VMEM((VTOK, D_VID), jnp.bfloat16),
                pltpu.VMEM((n_shard, ITOK, D_IR // n_shard), jnp.bfloat16),
                pltpu.VMEM((D_VID, GW), jnp.bfloat16),
                pltpu.VMEM((n_shard, D_IR // n_shard, GW), jnp.bfloat16),
                pltpu.VMEM((QPK, BLK, 2 * HEAD_DIM), jnp.bfloat16),
                pltpu.VMEM((QPK, BLK, HEAD_DIM), jnp.float32),
                pltpu.VMEM((QPK, BLK, 2 * HEAD_DIM), jnp.float32),
                dma((n_ctx, 3)),
                dma((2, 4, 2)),
                dma((2, 4, 2)),
                dma((2, 4, 2)),
                dma((2, 2, 2)),
                dma((2, n_shard)),
                dma((2, n_shard)),
                dma((2, 2, 2, n_shard)),
                dma((2, 2, n_shard)),
                dma((2, 2, n_shard)),
                dma((6,)),
            ],
            compiler_params=pltpu.CompilerParams(
                collective_id=0, has_side_effects=True, vmem_limit_bytes=48 * 1024 * 1024
            ),
            name="joint",
        )(vf, irf, jnp.transpose(wv, (1, 0, 2)), jnp.transpose(wi, (1, 0, 2)), tq, tk, tv, counts, mask)

    return jax.shard_map(
        shards,
        mesh=mesh,
        in_specs=(
            P("ctx", ("section", "tp")),
            P("ctx", ("section", "tp")),
            P(("section", "tp"), None, None),
            P(("section", "tp"), None, None),
            P("ctx", ("section", "tp")),
            P("ctx", ("section", "tp")),
            P("ctx", ("section", "tp")),
            P(),
            P(),
        ),
        out_specs=P("ctx", ("section", "tp")),
        check_vma=False,
    )
```

```python
import functools

import jax
import jax.numpy as jnp
from jax import lax
from jax.experimental import pallas as pl
from jax.experimental.pallas import tpu as pltpu
from jax.sharding import PartitionSpec as P

HEAD_DIM = 128
D_VID = 1024
D_IR = 768
VTOK = 128
ITOK = 32
ENC = VTOK + ITOK
XTOK = 96
QPK = 4
QW = QPK * HEAD_DIM
GW = 768
KVW = 2 * HEAD_DIM
BLK = 256
PAIR = 2 * BLK

LN_EPSILON = 1e-05
NEG_LARGE = -1e30
LOG2E = 1.4426950408889634
MESH = pl.DeviceIdType.MESH

PIECES = ((ENC, XTOK), (0, ENC), (0, BLK))
TEXT, ENCODED, WHOLE = 0, 1, 2
PROJ_TICK = 4
OFFSETS = (0, PROJ_TICK)
LAG = 1


def kernel(
    n_section,
    n_ctx,
    n_tp,
    vf_ref,
    if_ref,
    w_ref,
    tq_ref,
    tk_ref,
    tv_ref,
    counts_ref,
    mask_ref,
    out_ref,
    kv,
    bias,
    feats,
    wb,
    qa,
    top,
    acc,
    kv_recv,
    own_recv,
    own_send,
    z_send,
    core_send,
    y_send,
    x_recv,
    x_send,
    w_recv,
    w_send,
    w_fwd,
    local_sem,
):
    section = lax.axis_index("section")
    ctx = lax.axis_index("ctx")
    tp = lax.axis_index("tp")
    n_z = n_ctx // 4
    half = n_z // 2
    row = ctx // (2 * n_z)
    z = (ctx // 2) % n_z
    core = ctx % 2
    shard = section * n_tp + tp
    n_shard = n_section * n_tp

    def frame_at(r, zz, k):
        return r * (2 * n_z) + zz * 2 + k

    core_peer = {"ctx": frame_at(row, z, 1 - core)}
    y_peer = {"ctx": frame_at(1 - row, z, core)}
    up = {"ctx": frame_at(row, (z + 1) % n_z, core)}
    down = {"ctx": frame_at(row, (z + n_z - 1) % n_z, core)}
    z_next = {"ctx": frame_at(row, (z + 1 + core * (n_z - 2)) % n_z, core)}
    reach = half - core
    others = [(a, b) for a in range(n_section) for b in range(n_tp) if (a, b) != (0, 0)]

    def feature_peer(a, b):
        return {"section": (section + a) % n_section, "tp": (tp + b) % n_tp}

    def weight_peer(a, b):
        peer = feature_peer(a, b)
        if b:
            peer["ctx"] = frame_at(1 - row, z, core)
        return peer

    def shard_of(a, b):
        return ((section + a) % n_section) * n_tp + (tp + b) % n_tp

    barrier = pltpu.get_barrier_semaphore()
    greeted = [core_peer, y_peer, up, down]
    greeted += [feature_peer(a, b) for a, b in others]
    greeted += [weight_peer(a, b) for a, b in others if b]
    for peer in greeted:
        pl.semaphore_signal(barrier, inc=1, device_id=peer, device_id_type=MESH)

    w_rows = w_ref.shape[1]
    w_half = w_rows // 2
    d_ir = D_IR // n_shard
    my_half = pl.ds(pl.multiple_of(core * w_half, w_half), w_half)
    locals_ = [
        pltpu.make_async_copy(vf_ref, feats.at[shard, pl.ds(0, VTOK)], local_sem.at[0]),
        pltpu.make_async_copy(tv_ref, kv.at[ctx, pl.ds(ENC, XTOK), pl.ds(HEAD_DIM, HEAD_DIM)], local_sem.at[1]),
        pltpu.make_async_copy(tk_ref, kv.at[ctx, pl.ds(ENC, XTOK), pl.ds(0, HEAD_DIM)], local_sem.at[2]),
        pltpu.make_async_copy(w_ref.at[shard, my_half], wb.at[shard, my_half], local_sem.at[3]),
    ]
    for copy in locals_:
        copy.start()
    feats[shard, VTOK:, :d_ir] = if_ref[...]

    def remote(src, dst, send_sem, recv_sem, peer):
        return pltpu.make_async_remote_copy(
            src_ref=src, dst_ref=dst, send_sem=send_sem, recv_sem=recv_sem, device_id=peer, device_id_type=MESH
        )

    def feature_send(n):
        return remote(feats.at[shard], feats.at[shard], x_send.at[n], x_recv.at[shard], feature_peer(*others[n]))

    def feature_arrival(n):
        place = feats.at[shard_of(*others[n])]
        return remote(place, place, x_send.at[n], x_recv.at[shard_of(*others[n])], core_peer)

    parts = (pl.ds(QW, KVW), pl.ds(0, QW))

    def weight_send(n, part):
        a, b = others[n]
        return remote(
            w_ref.at[shard_of(a, b), my_half, parts[part]],
            wb.at[shard, my_half, parts[part]],
            w_send.at[part, n],
            w_recv.at[part, shard],
            weight_peer(a, b),
        )

    def weight_arrival(n, part):
        src = shard_of(*others[n])
        place = wb.at[src, my_half, parts[part]]
        return remote(place, place, w_send.at[part, n], w_recv.at[part, src], core_peer)

    def weight_forward(part, k):
        place = wb.at[:, pl.ds(pl.multiple_of(k * w_half, w_half), w_half), parts[part]]
        return remote(place, place, w_fwd.at[0, part], w_fwd.at[1, part], core_peer)

    def own_swap(piece, k):
        first, count = PIECES[piece]
        place = kv.at[frame_at(row, z, k), pl.ds(first, count)]
        return remote(place, place, own_send.at[piece], own_recv.at[piece], core_peer)

    def pair_copy(r, zz, piece, sem, peer):
        first, count = PIECES[piece]
        place = kv.at[pl.ds(frame_at(r, zz, 0), 2), pl.ds(first, count)]
        return remote(place, place, sem, kv_recv.at[r * n_z + zz, piece], peer)

    def arrived(r, zz, piece):
        pair_copy(r, zz, piece, z_send.at[0, 0], core_peer).wait_recv()

    def z_of(way, distance):
        return (z + n_z + (2 * way - 1) * distance) % n_z

    def act(copy, start):
        if start:
            copy.start()
        else:
            copy.wait_send()

    def line_step(tick, piece, start):
        distance = tick - OFFSETS[piece]
        slot = tick % 2
        zz = z_of(core, distance)
        wanted = (row == 0) | ((core == 0) & (distance <= z)) | ((core == 1) & (zz < half - 1))
        goes_on = (row == 0) | (core == 1) | (z < n_z - 1)

        @pl.when((distance >= 0) & (distance <= reach) & wanted)
        def _():
            if start:
                @pl.when(distance >= 1)
                def _():
                    arrived(row, zz, piece)

            @pl.when((distance < reach) & goes_on)
            def _():
                act(pair_copy(row, zz, piece, z_send.at[piece, slot], z_next), start)

            @pl.when((row == 0) & (distance == 0) if piece == TEXT else row == 0)
            def _():
                act(pair_copy(row, zz, piece, y_send.at[piece, slot], y_peer), start)

    def text_step(tick, start):
        distance = tick - 1
        slot = tick % 2
        zz = z_of(core, distance)

        @pl.when((row == 1) & (distance >= 0) & (distance <= reach))
        def _():
            if start:
                arrived(0, zz, TEXT)

            @pl.when(distance < reach)
            def _():
                act(pair_copy(0, zz, TEXT, z_send.at[2, slot], z_next), start)

    def whole_step(tick, own, start):
        distance = tick - PROJ_TICK if own else tick - PROJ_TICK - 1
        slot = tick % 2
        zz = z_of(core, distance)
        if own:
            active = (distance >= 1) & (distance <= reach) & (zz < z)
        else:
            active = (row == 1) & (distance >= 0) & (distance <= reach)

        @pl.when(active)
        def _():
            if start and not own:
                arrived(0, zz, ENCODED)

            @pl.when(distance >= 1)
            def _():
                act(pair_copy(row if own else 0, zz, WHOLE, core_send.at[int(own), slot], core_peer), start)

    def lines(tick, start=True):
        line_step(tick, ENCODED, start)
        line_step(tick, TEXT, start)
        text_step(tick, start)

    def wholes(tick, start=True):
        whole_step(tick, True, start)
        whole_step(tick, False, start)

    def step(tick):
        lines(tick - 2, start=False)
        lines(tick)
        wholes(tick - 2, start=False)
        wholes(tick)

    def attend(first_frame, diagonal):
        rows = pl.ds(pl.multiple_of(first_frame * BLK, PAIR), PAIR)
        pair = kv[pl.ds(first_frame, 2)].reshape(PAIR, KVW)
        keys = jnp.concatenate([pair[:, :HEAD_DIM], bias[rows, :]], axis=1)
        values = jnp.concatenate([pair[:, HEAD_DIM:], jnp.ones((PAIR, HEAD_DIM), jnp.bfloat16)], axis=1)
        for h in range(QPK):
            scores = lax.dot_general(
                qa[h], keys, (((1,), (1,)), ((), ())), preferred_element_type=jnp.float32
            )
            if diagonal:
                key_slot = lax.broadcasted_iota(jnp.int32, (BLK, PAIR), 1)
                query_slot = lax.broadcasted_iota(jnp.int32, (BLK, PAIR), 0) + core * BLK
                scores = jnp.where(key_slot <= query_slot, scores, NEG_LARGE)
            old = top[h]
            new = jnp.maximum(old, jnp.max(scores, axis=1, keepdims=True))
            top[h] = new
            weights = jnp.concatenate(
                [jnp.exp2(scores[:, i : i + HEAD_DIM] - new) for i in range(0, PAIR, HEAD_DIM)], axis=1
            ).astype(jnp.bfloat16)
            factor = jnp.exp2(old - new)
            acc[h] = acc[h] * jnp.concatenate([factor, factor], axis=1) + jnp.dot(
                weights, values, preferred_element_type=jnp.float32
            )

    def first_at(turn):
        return jnp.where(turn < LAG, 2 * turn, turn + LAG)

    def compute(turn, part):
        low, high = first_at(turn), jnp.where(turn < 0, 0, first_at(turn + 1))

        def item(n, _):
            distance = low + n // 2
            way, r = part, n % 2
            zz = z_of(way, distance)
            present = (turn >= 0) & (r <= row) & (distance < high) & (distance <= half)
            if way == 1:
                present = present & (distance >= 1) & (distance < half)
            present = present & jnp.logical_not((r == row) & (distance == 0))

            @pl.when(present & ((r < row) | (zz < z)))
            def _():
                @pl.when((core != part) & (distance >= 1))
                def _():
                    arrived(r, zz, WHOLE)

                attend(frame_at(r, zz, 0), False)

            return 0

        lax.fori_loop(0, 4, item, 0)

    pl.semaphore_wait(barrier, len(greeted))
    locals_[0].wait()
    for n in range(len(others)):
        feature_send(n).start()
    locals_[1].wait()
    locals_[2].wait()
    own_swap(TEXT, core).start()
    for n in range(len(others)):
        weight_send(n, 0).start()
    own_swap(TEXT, 1 - core).wait_recv()
    lines(0)
    for n in range(len(others)):
        weight_send(n, 1).start()

    def mask_frame(f, _):
        seen = mask_ref[ctx, f]
        video_live = counts_ref[0, f] * seen
        ir_live = counts_ref[1, f] * seen
        text_live = XTOK * seen
        base = pl.multiple_of(f * BLK, BLK)
        for first, count, live in ((0, VTOK, video_live), (VTOK, ITOK, ir_live), (ENC, XTOK, text_live)):
            slot = lax.broadcasted_iota(jnp.int32, (count, HEAD_DIM), 0)
            bias[pl.ds(base + first, count), :] = jnp.where(slot < live, 0.0, NEG_LARGE).astype(jnp.bfloat16)
        return 0

    lax.fori_loop(0, n_ctx, mask_frame, 0)

    for h in range(QPK):
        lane = lax.broadcasted_iota(jnp.int32, (BLK, HEAD_DIM), 1)
        qa[h, :, HEAD_DIM:] = jnp.where(lane == 0, 1.0, 0.0).astype(jnp.bfloat16)
        top[h] = jnp.full((BLK, HEAD_DIM), NEG_LARGE, jnp.float32)
        acc[h] = jnp.zeros((BLK, 2 * HEAD_DIM), jnp.float32)

    def early(tick, _):
        step(tick)
        return 0

    lax.fori_loop(1, PROJ_TICK, early, 0)

    for n in range(len(others)):
        feature_arrival(n).wait_recv()
    for n in range(len(others)):
        feature_send(n).wait_send()

    def norm_terms(values, count):
        center = sum(jnp.sum(x, axis=1, keepdims=True) for x in values) / count
        spread = sum(jnp.sum(x * x, axis=1, keepdims=True) for x in values) / count - center * center
        return center, lax.rsqrt(spread + LN_EPSILON)

    video = [feats[n, :VTOK].astype(jnp.float32) for n in range(n_shard)]
    center, gain = norm_terms(video, D_VID)
    for n in range(n_shard):
        feats[n, :VTOK] = ((video[n] - center) * gain).astype(jnp.bfloat16)
    infra = [feats[n, VTOK:, :d_ir].astype(jnp.float32) for n in range(n_shard)]
    center, gain = norm_terms(infra, D_IR)
    for n in range(n_shard):
        feats[n, VTOK:, :d_ir] = ((infra[n] - center) * gain).astype(jnp.bfloat16)

    def take_weights(part):
        for n in range(len(others)):
            weight_arrival(n, part).wait_recv()
        weight_forward(part, core).start()
        weight_forward(part, 1 - core).wait_recv()

    def project(columns):
        d_vid = w_rows - d_ir
        rows = jnp.concatenate([feats[n, :VTOK] for n in range(n_shard)], axis=1)
        maps = jnp.concatenate([wb[n, :d_vid, columns] for n in range(n_shard)], axis=0)
        video_out = jnp.dot(rows, maps, preferred_element_type=jnp.float32)
        ir_out = sum(
            jnp.dot(feats[n, VTOK:, :d_ir], wb[n, d_vid:, columns], preferred_element_type=jnp.float32)
            for n in range(n_shard)
        )
        return video_out, ir_out

    locals_[3].wait()
    take_weights(0)
    video_out, ir_out = project(slice(QW, GW))
    kv[ctx, :VTOK, :] = video_out.astype(jnp.bfloat16)
    kv[ctx, VTOK:ENC, :] = ir_out.astype(jnp.bfloat16)
    own_swap(ENCODED, core).start()
    own_swap(ENCODED, 1 - core).wait_recv()

    lax.fori_loop(PROJ_TICK, PROJ_TICK + 2 + LAG, early, 0)

    take_weights(1)
    scale = HEAD_DIM ** (-0.5) * LOG2E
    video_out, ir_out = project(slice(0, QW))
    for h in range(QPK):
        columns = slice(h * HEAD_DIM, (h + 1) * HEAD_DIM)
        qa[h, :VTOK, :HEAD_DIM] = (video_out[:, columns] * scale).astype(jnp.bfloat16)
        qa[h, VTOK:ENC, :HEAD_DIM] = (ir_out[:, columns] * scale).astype(jnp.bfloat16)
        qa[h, ENC:, :HEAD_DIM] = (tq_ref[:, columns].astype(jnp.float32) * scale).astype(jnp.bfloat16)

    attend(frame_at(row, z, 0), True)

    def late(tick, _):
        turn = tick - PROJ_TICK - 2 - LAG
        lines(tick - 2, start=False)
        lines(tick)
        compute(turn, 0)
        wholes(tick - 2, start=False)
        wholes(tick)
        compute(turn, 1)
        return 0

    last = half + PROJ_TICK + 3
    lax.fori_loop(PROJ_TICK + 2 + LAG, last, late, 0)

    for h in range(QPK):
        out_ref[:, h * HEAD_DIM : (h + 1) * HEAD_DIM] = (
            acc[h, :, :HEAD_DIM] / acc[h, :, HEAD_DIM:]
        ).astype(jnp.bfloat16)

    for tick in (last - 2, last - 1):
        lines(tick, start=False)
        wholes(tick, start=False)
    own_swap(TEXT, core).wait_send()
    own_swap(ENCODED, core).wait_send()
    for part in range(2):
        weight_forward(part, core).wait_send()
        for n in range(len(others)):
            weight_send(n, part).wait_send()


def solution(mesh):
    n_section, n_ctx, n_tp = mesh.shape["section"], mesh.shape["ctx"], mesh.shape["tp"]
    n_shard = n_section * n_tp

    def shards(vf, irf, wv, wi, tq, tk, tv, counts, mask):
        anywhere = pl.BlockSpec(memory_space=pl.ANY)
        vmem = pl.BlockSpec(memory_space=pltpu.VMEM)
        smem = pl.BlockSpec(memory_space=pltpu.SMEM)
        dma = pltpu.SemaphoreType.DMA
        adapters = jnp.concatenate([jnp.transpose(wv, (1, 0, 2)), jnp.transpose(wi, (1, 0, 2))], axis=1)
        return pl.pallas_call(
            functools.partial(kernel, n_section, n_ctx, n_tp),
            out_shape=jax.ShapeDtypeStruct((BLK, QW), jnp.bfloat16),
            in_specs=[anywhere, vmem, anywhere, vmem] + [anywhere] * 2 + [smem] * 2,
            out_specs=vmem,
            scratch_shapes=[
                pltpu.VMEM((n_ctx, BLK, KVW), jnp.bfloat16),
                pltpu.VMEM((n_ctx * BLK, HEAD_DIM), jnp.bfloat16),
                pltpu.VMEM((n_shard, ENC, D_VID // n_shard), jnp.bfloat16),
                pltpu.VMEM((n_shard, (D_VID + D_IR) // n_shard, GW), jnp.bfloat16),
                pltpu.VMEM((QPK, BLK, 2 * HEAD_DIM), jnp.bfloat16),
                pltpu.VMEM((QPK, BLK, HEAD_DIM), jnp.float32),
                pltpu.VMEM((QPK, BLK, 2 * HEAD_DIM), jnp.float32),
                dma((n_ctx // 2, 3)),
                dma((2,)),
                dma((2,)),
                dma((3, 2)),
                dma((2, 2)),
                dma((2, 2)),
                dma((n_shard,)),
                dma((n_shard,)),
                dma((2, n_shard)),
                dma((2, n_shard)),
                dma((2, 2)),
                dma((4,)),
            ],
            compiler_params=pltpu.CompilerParams(
                collective_id=0, has_side_effects=True, vmem_limit_bytes=48 * 1024 * 1024
            ),
            name="joint",
        )(vf, irf, adapters, tq, tk, tv, jnp.transpose(counts), mask)

    return jax.shard_map(
        shards,
        mesh=mesh,
        in_specs=(
            P("ctx", ("section", "tp")),
            P("ctx", ("section", "tp")),
            P(("section", "tp"), None, None),
            P(("section", "tp"), None, None),
            P("ctx", ("section", "tp")),
            P("ctx", ("section", "tp")),
            P("ctx", ("section", "tp")),
            P(),
            P(),
        ),
        out_specs=P("ctx", ("section", "tp")),
        check_vma=False,
    )
```
